256 devices in a mesh: view: 2 (over core), sky: 128 (over z, x, y).
Axes of the slice: x: 4, y: 4, z: 8, core: 2. Of those that a mesh axis runs over, the one named last changes fastest.
Arguments:
- pixels: bfloat16 [2, 262144, 128], P('view', 'sky'), may hold values from -6 to 6
- cotangent: bfloat16 [2, 262144, 128], P('view', 'sky'), may hold values from -6 to 6
- filters: bfloat16 [4, 128, 128], replicated, may hold values from -0.25 to 0.25
- lap_tiles: bfloat16 [128, 24, 256, 256], P('sky'), may hold values from -0.15625 to 0.15625
- tile_target: int32 [128, 24], P('sky'), may hold values from 0 to 7
- tile_source: int32 [128, 24], P('sky'), may hold values from 0 to 15
- tile_count: int32 [128], P('sky'), may hold values from 12 to 24, as said below
- send_blocks: int32 [128, 4, 2], P('sky'), may hold values from 0 to 7
Outputs:
- outputs: bfloat16 [2, 262144, 128], P('view', 'sky')
- pixel_grad: bfloat16 [2, 262144, 128], P('view', 'sky')
- filter_grad: float32 [4, 128, 128], replicated
The draws below stay inside these ranges and needn't reach their ends.
Inputs may be any that keep to these rules, and one draw needn't show every extreme that they name: `tile_count`: every device has at least half of 24 live tiles, and some device has exactly 24. `tile_source`: indices below 8 are own blocks, the others received ones.
All inputs are finite; a program needn't handle non-finite values.
Results may differ from the reference program's by a relative error of at most 0.017.
Values may be sent and summed in bfloat16 or wider, within the bound.
No kernel may reach another device: no remote copies, remote signals or barrier semaphores. Data moves between devices by JAX's collectives and lax.ppermute only.
A program may use at most 64 MiB of HBM per device.

```python
import math
import jax
import jax.numpy as jnp
from jax import lax

C = 128
BLK = 256
K = 4
NB = 8
NSEND = 2
MAXT = 24
NEXT = 16
SKY_DEVS = 128
VIEWS = 2
NPIX = 262144


def draw_tile_count(key, part):
    counts = jax.random.randint(key, (SKY_DEVS,), MAXT // 2, MAXT + 1)
    chosen = jax.random.randint(jax.random.fold_in(key, 7), (), 0, SKY_DEVS)
    return counts.at[chosen].set(MAXT).astype(jnp.int32)


def with_ends(values, rng, least, top_value):
    longest = values.shape.index(max(values.shape))
    spots = []
    for shift in (0, 1):
        where = [jax.random.randint(jax.random.fold_in(rng, axis), (), 0, length) for axis, length in enumerate(values.shape)]
        where[longest] = (where[longest] + shift) % values.shape[longest]
        spots.append(tuple(where))
    return values.at[spots[0]].set(least).at[spots[1]].set(top_value)


def block_scale(stream_key, extent, cuts, least, largest):
    loudness = 1.0
    for axis_at, parts in cuts:
        steps = jax.random.uniform(jax.random.fold_in(jax.random.fold_in(stream_key, 6), axis_at), (parts,), jnp.float32, least / len(cuts), largest / len(cuts))
        loudness = loudness * jnp.repeat(jnp.exp(steps), extent[axis_at] // parts).reshape((-1,) + (1,) * (len(extent) - 1 - axis_at))
    return loudness


def bell_draw(key, shape, deviation, most, cuts=(), kind=jnp.bfloat16):
    factor_of = block_scale(key, shape, cuts, -0.22, 0.18) if cuts else 1.0
    entries = jax.random.normal(key, shape, jnp.float32) * deviation * factor_of
    return jnp.minimum(jnp.maximum(entries, -most), most).astype(kind)


def setup_inputs(seed: int = 0) -> dict:
    keys = jax.random.split(jax.random.key(seed), 9)
    return {
        "pixels": bell_draw(keys[0], (VIEWS, NPIX, C), 1.0, 6.0, ((0, 2), (1, 128))),
        "cotangent": bell_draw(keys[1], (VIEWS, NPIX, C), 1.0, 6.0, ((0, 2), (1, 128))),
        "filters": bell_draw(keys[2], (K, C, C), (K * C) ** -0.5, 0.25),
        "lap_tiles": bell_draw(keys[3], (SKY_DEVS, MAXT, BLK, BLK), (6 * BLK) ** -0.5, 0.15625, ((0, 128),)),
        "tile_target": with_ends(jax.random.randint(keys[4], (SKY_DEVS, MAXT), 0, NB), jax.random.fold_in(keys[4], 1), 0, NB - 1).astype(jnp.int32),
        "tile_source": with_ends(jax.random.randint(keys[5], (SKY_DEVS, MAXT), 0, NEXT), jax.random.fold_in(keys[5], 1), 0, NEXT - 1).astype(jnp.int32),
        "tile_count": draw_tile_count(jax.random.fold_in(keys[8], 71), 0),
        "send_blocks": with_ends(jax.random.randint(keys[7], (SKY_DEVS, 4, NSEND), 0, NB), jax.random.fold_in(keys[7], 1), 0, NB - 1).astype(jnp.int32),
    }


OFFSETS = (1, -1, 2, -2)

def shifted(values, offset):
    filler = jnp.zeros((abs(offset),) + values.shape[1:], values.dtype)
    if offset > 0:
        return jnp.concatenate([filler, values[:-offset]], axis=0)
    return jnp.concatenate([values[-offset:], filler], axis=0)

def extend(blocks, send_blocks):
    pieces = [blocks]
    for number, offset in enumerate(OFFSETS):
        picked = jax.vmap(lambda source, chosen: source[chosen])(blocks, send_blocks[:, number])
        pieces.append(shifted(picked, offset))
    return jnp.concatenate(pieces, axis=1)

def forward_pass(blocks, lap_tiles, tile_target, tile_source, tile_count, send_blocks):
    extended = extend(blocks, send_blocks)

    def one_device(operands):
        tile_set, target, source, live_count, ext_blocks = operands
        gathered = ext_blocks[source].astype(jnp.float32)
        products = jnp.einsum('tpq,tqc->tpc', tile_set.astype(jnp.float32), gathered)
        live_mask = jnp.arange(MAXT) < live_count
        routing = ((target[None, :] == jnp.arange(NB)[:, None]) & live_mask[None, :]).astype(jnp.float32)
        return jnp.einsum('bt,tpc->bpc', routing, products)
    return lax.map(one_device, (lap_tiles, tile_target, tile_source, tile_count, extended))

def transposed_pass(blocks, lap_tiles, tile_target, tile_source, tile_count, send_blocks):

    def one_device(operands):
        tile_set, target, source, live_count, own_blocks = operands
        picked = own_blocks[target].astype(jnp.float32)
        products = jnp.einsum('tpq,tpc->tqc', tile_set.astype(jnp.float32), picked)
        live_mask = jnp.arange(MAXT) < live_count
        routing = ((source[None, :] == jnp.arange(NEXT)[:, None]) & live_mask[None, :]).astype(jnp.float32)
        return jnp.einsum('et,tqc->eqc', routing, products)
    slot_sums = lax.map(one_device, (lap_tiles, tile_target, tile_source, tile_count, blocks))
    combined = slot_sums[:, :NB]
    for number, offset in enumerate(OFFSETS):
        begin = NB + number * NSEND
        back = shifted(slot_sums[:, begin:begin + NSEND], -offset)
        routing = (send_blocks[:, number, None, :] == jnp.arange(NB)[None, :, None]).astype(jnp.float32)
        combined = combined + jnp.einsum('dbj,djqc->dbqc', routing, back)
    return combined

def reference(pixels, cotangent, filters, lap_tiles, tile_target, tile_source, tile_count, send_blocks):
    graph = (lap_tiles, tile_target, tile_source, tile_count, send_blocks)
    outputs = []
    adjoints = []
    filter_sum = jnp.zeros((K, C, C), jnp.float32)
    for view in range(VIEWS):
        base = pixels[view].reshape(SKY_DEVS, NB, BLK, C)
        cheb_one = forward_pass(base, *graph).astype(jnp.bfloat16)
        cheb_two = (2.0 * forward_pass(cheb_one, *graph) - base.astype(jnp.float32)).astype(jnp.bfloat16)
        cheb_three = (2.0 * forward_pass(cheb_two, *graph) - cheb_one.astype(jnp.float32)).astype(jnp.bfloat16)
        flattened = [member.reshape(NPIX, C) for member in (base, cheb_one, cheb_two, cheb_three)]
        result = jnp.dot(flattened[0], filters[0], preferred_element_type=jnp.float32)
        for order in range(1, K):
            result = result + jnp.dot(flattened[order], filters[order], preferred_element_type=jnp.float32)
        outputs.append(result.astype(jnp.bfloat16))
        upstream = cotangent[view]
        pulled = [jnp.dot(upstream, filters[order].T, preferred_element_type=jnp.float32).reshape(SKY_DEVS, NB, BLK, C) for order in range(K)]
        adj_three = pulled[3]
        adj_two = pulled[2] + 2.0 * transposed_pass(adj_three.astype(jnp.bfloat16), *graph)
        adj_one = pulled[1] + 2.0 * transposed_pass(adj_two.astype(jnp.bfloat16), *graph) - adj_three
        adj_zero = pulled[0] + transposed_pass(adj_one.astype(jnp.bfloat16), *graph) - adj_two
        adjoints.append(adj_zero.reshape(NPIX, C).astype(jnp.bfloat16))
        filter_sum = filter_sum + jnp.stack([jnp.dot(flattened[order].T, upstream, preferred_element_type=jnp.float32) for order in range(K)])
    scale = 1.0 / math.sqrt(VIEWS * NPIX)
    return (jnp.stack(outputs), jnp.stack(adjoints), filter_sum * scale)
```

```python
import math

import jax
import jax.numpy as jnp
from jax import lax
from jax.experimental import pallas as pl
from jax.experimental.pallas import tpu as pltpu
from jax.sharding import PartitionSpec as P

OFFSETS = (1, -1, 2, -2)
START_ORDER = (2, 3, 0, 1)
F32 = jnp.float32
BF16 = jnp.bfloat16
ANY = pl.BlockSpec(memory_space=pl.ANY)
VMEM = pl.BlockSpec(memory_space=pltpu.VMEM)
SMEM = pl.BlockSpec(memory_space=pltpu.SMEM)
NB, BLK, C, MAXT, NSEND = 8, 256, 128, 24, 2
NEXT = NB + 4 * NSEND


def mm(a, b):
    return jnp.dot(a, b, preferred_element_type=F32)


def call(kernel, name, outs, out_specs, in_specs, scratch, flops, args):
    size = sum(math.prod(o.shape) * o.dtype.itemsize for o in outs)
    size += sum(math.prod(a.shape) * a.dtype.itemsize for a in args)
    return pl.pallas_call(
        kernel,
        name=name,
        out_shape=outs,
        in_specs=in_specs,
        out_specs=out_specs,
        scratch_shapes=scratch,
        cost_estimate=pl.CostEstimate(flops=flops, bytes_accessed=size, transcendentals=0),
        compiler_params=pltpu.CompilerParams(vmem_limit_bytes=24 * 1024 * 1024),
    )(*args)


def start_tiles(tiles, tile_buf, tile_sem):
    copies = [pltpu.make_async_copy(tiles.at[t], tile_buf.at[t], tile_sem.at[t]) for t in range(MAXT)]
    for copy in copies:
        copy.start()
    return copies


PIECE = jax.ShapeDtypeStruct((NSEND, BLK, C), BF16)
PIECE_T = jax.ShapeDtypeStruct((NSEND, C, BLK), BF16)
BLOCKS = jax.ShapeDtypeStruct((NB, BLK, C), BF16)
BLOCKS_T = jax.ShapeDtypeStruct((NB, C, BLK), BF16)
OWN_T = jax.ShapeDtypeStruct((NB, C, BLK), F32)
TILE_SCRATCH = [pltpu.VMEM((MAXT, BLK, BLK), BF16), pltpu.SemaphoreType.DMA((MAXT,))]
STEP_FLOPS = 2 * MAXT * BLK * BLK * C


def pick_kernel(send, blocks, *rest):
    outs, sem = rest[:4], rest[4]
    copies = []
    for i in range(4):
        for j in range(NSEND):
            copies.append(
                pltpu.make_async_copy(blocks.at[send[0, i, j]], outs[i].at[j], sem.at[i * NSEND + j])
            )
    for copy in copies:
        copy.start()
    for copy in copies:
        copy.wait()


def pick(send, blocks):
    return call(
        pick_kernel, "pick", [PIECE] * 4, [ANY] * 4, [SMEM, ANY],
        [pltpu.SemaphoreType.DMA((4 * NSEND,))], 0, (send, blocks),
    )


def forward_kernel(first, last, *refs):
    refs = list(refs)
    take = lambda n: [refs.pop(0) for _ in range(n)]
    target, source, count, send, tiles, blocks = take(6)
    arrived = take(4)
    before = None if first else take(1)[0]
    if last:
        base, filters = take(2)
        (out,) = take(1)
    else:
        (out,) = take(1)
        pieces = take(4)
    tile_buf, tile_sem, ext, ext_sem, acc = take(5)
    tile_copies = start_tiles(tiles, tile_buf, tile_sem)
    ext_copies = [pltpu.make_async_copy(blocks, ext.at[pl.ds(0, NB)], ext_sem.at[0])]
    for i in range(4):
        ext_copies.append(
            pltpu.make_async_copy(
                arrived[i], ext.at[pl.ds(NB + i * NSEND, NSEND)], ext_sem.at[1 + i]
            )
        )
    for copy in ext_copies:
        copy.start()
    acc[...] = jnp.zeros_like(acc)
    for copy in ext_copies:
        copy.wait()
    for t in range(MAXT):
        tile_copies[t].wait()
        where = jnp.where(t < count[0], target[0, t], NB)
        acc[where] += mm(tile_buf[t], ext[source[0, t]])
    for b in range(NB):
        value = acc[b]
        if not first:
            value = 2.0 * value - before[b].astype(F32)
        value = value.astype(BF16)
        if last:
            result = mm(base[b], filters[0]) + mm(before[b], filters[1])
            result = result + mm(ext[b], filters[2]) + mm(value, filters[3])
            out[b] = result.astype(BF16)
        else:
            out[b] = value
    if not last:
        for i in range(4):
            for j in range(NSEND):
                pieces[i][j] = out[send[0, i, j]]


def forward(tables, send, tiles, blocks, arrived, before=None, base=None, filters=None):
    first, last = before is None, base is not None
    args = [*tables, send, tiles, blocks, *arrived]
    specs = [SMEM] * 4 + [ANY] * 6
    if not first:
        args.append(before)
        specs.append(VMEM)
    if last:
        args += [base, filters]
        specs += [VMEM, VMEM]
        outs, out_specs = [BLOCKS], [VMEM]
    else:
        outs, out_specs = [BLOCKS] + [PIECE] * 4, [VMEM] * 5
    scratch = TILE_SCRATCH + [
        pltpu.VMEM((NEXT, BLK, C), BF16),
        pltpu.SemaphoreType.DMA((5,)),
        pltpu.VMEM((NB + 1, BLK, C), F32),
    ]
    kernel = lambda *refs: forward_kernel(first, last, *refs)
    return call(kernel, "forward", outs, out_specs, specs, scratch, STEP_FLOPS, args)


def push_terms(target, source, count, tile_copies, tile_buf, held, acc, own, pieces):
    acc[...] = jnp.zeros_like(acc)
    for t in range(MAXT):
        tile_copies[t].wait()
        where = jnp.where(t < count[0], source[0, t], NEXT)
        acc[where] += mm(held[target[0, t]], tile_buf[t])
    for i in range(4):
        for j in range(NSEND):
            pieces[i][j] = acc[NB + i * NSEND + j].astype(BF16)
    own[...] = acc[0:NB]


def adjoint_start_kernel(target, source, count, tiles, upstream, held, own, *rest):
    pieces = rest[:4]
    tile_buf, tile_sem, acc = rest[4:]
    tile_copies = start_tiles(tiles, tile_buf, tile_sem)
    for b in range(NB):
        held[b] = upstream[b].astype(F32).T.astype(BF16)
    push_terms(target, source, count, tile_copies, tile_buf, held, acc, own, pieces)


ACC_T = pltpu.VMEM((NEXT + 1, C, BLK), F32)


def adjoint_start(tables, tiles, upstream):
    return call(
        adjoint_start_kernel, "adjoint_start", [BLOCKS_T, OWN_T] + [PIECE_T] * 4, [VMEM] * 6,
        [SMEM] * 3 + [ANY, VMEM], TILE_SCRATCH + [ACC_T], STEP_FLOPS, (*tables, tiles, upstream),
    )


def gather_terms(send, own, arrived, total):
    total[...] = own[...]
    for i in range(4):
        for j in range(NSEND):
            total[send[0, i, j]] += arrived[i][j].astype(F32)


def adjoint_kernel(first, *refs):
    refs = list(refs)
    take = lambda n: [refs.pop(0) for _ in range(n)]
    target, source, count, send, tiles, own_in = take(6)
    arrived = take(4)
    before = None if first else take(1)[0]
    held, own = take(2)
    pieces = take(4)
    tile_buf, tile_sem, acc = take(3)
    tile_copies = start_tiles(tiles, tile_buf, tile_sem)
    total = acc.at[pl.ds(0, NB)]
    gather_terms(send, own_in, arrived, total)
    for b in range(NB):
        value = total[b]
        if not first:
            value = 2.0 * value - before[b].astype(F32)
        held[b] = value.astype(BF16)
    push_terms(target, source, count, tile_copies, tile_buf, held, acc, own, pieces)


def adjoint(tables, send, tiles, own, arrived, before=None):
    first = before is None
    args = [*tables, send, tiles, own, *arrived] + ([] if first else [before])
    specs = [SMEM] * 4 + [ANY] + [VMEM] * (5 if first else 6)
    kernel = lambda *refs: adjoint_kernel(first, *refs)
    return call(
        kernel, "adjoint", [BLOCKS_T, OWN_T] + [PIECE_T] * 4, [VMEM] * 6, specs,
        TILE_SCRATCH + [ACC_T], STEP_FLOPS, args,
    )


def adjoint_end_kernel(send, own_in, a0, a1, a2, a3, u0, u1, u2, filters, out, total):
    gather_terms(send, own_in, (a0, a1, a2, a3), total)
    for b in range(NB):
        u3 = (2.0 * total[b] - u1[b].astype(F32)).astype(BF16)
        grad = mm(filters[0], u0[b]) + mm(filters[1], u1[b])
        grad = grad + mm(filters[2], u2[b]) + mm(filters[3], u3)
        out[b] = grad.T.astype(BF16)


def adjoint_end(send, own, arrived, us, filters):
    return call(
        adjoint_end_kernel, "adjoint_end", [BLOCKS], [VMEM], [SMEM] + [VMEM] * 9,
        [pltpu.VMEM((NB, C, BLK), F32)], 8 * NB * BLK * C * C, (send, own, *arrived, *us, filters),
    )[0]


def grads_kernel(base, one, two, u0, u1, out):
    g0 = jnp.zeros((C, C), F32)
    g1, g2, g3 = g0, g0, g0
    for b in range(NB):
        g0 += mm(u0[b], base[b])
        g1 += mm(u0[b], one[b])
        g2 += mm(u0[b], two[b])
        g3 += mm(u1[b], two[b])
    out[0] = g0.T
    out[1] = g1.T
    out[2] = g2.T
    out[3] = (2.0 * g3 - g1).T


def grads(base, one, two, u0, u1):
    return call(
        grads_kernel, "grads", [jax.ShapeDtypeStruct((4, C, C), F32)], [VMEM], [VMEM] * 5, [],
        8 * NB * BLK * C * C, (base, one, two, u0, u1),
    )[0]


def passed_along(array, by):
    size = lax.axis_size("sky")
    return lax.ppermute(array, "sky", [(i, i + by) for i in range(size) if 0 <= i + by < size])


def spread(pieces, sign):
    got = [None] * 4
    for i in START_ORDER:
        got[i] = passed_along(pieces[i], sign * OFFSETS[i])
    return got


def total_over_devices(local):
    axes = ("view", "sky")
    count = lax.axis_size("view") * lax.axis_size("sky")
    rows = local.shape[0] * local.shape[1] // count
    parts = lax.all_to_all(local.reshape(count, rows, C), axes, 0, 0, tiled=True)
    part = jnp.sum(parts, axis=0)
    whole = lax.all_to_all(jnp.broadcast_to(part[None], parts.shape), axes, 0, 0, tiled=True)
    return whole.reshape(local.shape)


def per_device(
    pixels, cotangent, filters, lap_tiles, tile_target, tile_source, tile_count, send_blocks
):
    base = pixels.reshape(NB, BLK, C)
    upstream = cotangent.reshape(NB, BLK, C)
    tiles = lap_tiles.reshape(MAXT, BLK, BLK)
    tables = (tile_target, tile_source, tile_count)
    send = send_blocks

    f1 = spread(pick(send, base), 1)
    u0, own, *terms = adjoint_start(tables, tiles, upstream)
    b1 = spread(terms, -1)
    one, *pieces = forward(tables, send, tiles, base, f1)
    f2 = spread(pieces, 1)
    u1, own, *terms = adjoint(tables, send, tiles, own, b1)
    b2 = spread(terms, -1)
    two, *pieces = forward(tables, send, tiles, one, f2, before=base)
    local = grads(base, one, two, u0, u1)
    summed = total_over_devices(local)
    f3 = spread(pieces, 1)
    u2, own, *terms = adjoint(tables, send, tiles, own, b2, before=u0)
    b3 = spread(terms, -1)
    (outputs,) = forward(tables, send, tiles, two, f3, before=one, base=base, filters=filters)
    pixel_grad = adjoint_end(send, own, b3, (u0, u1, u2), filters)
    scale = 1.0 / math.sqrt(lax.axis_size("view") * lax.axis_size("sky") * NB * BLK)
    return (outputs.reshape(pixels.shape), pixel_grad.reshape(pixels.shape), summed * scale)


def solution(mesh):
    return jax.shard_map(
        per_device,
        mesh=mesh,
        in_specs=(
            P("view", "sky", None),
            P("view", "sky", None),
            P(),
            P("sky", None, None, None),
            P("sky", None),
            P("sky", None),
            P("sky"),
            P("sky", None, None),
        ),
        out_specs=(P("view", "sky", None), P("view", "sky", None), P()),
        check_vma=False,
    )
```

```python
import math

import jax
import jax.numpy as jnp
from jax import lax
from jax.experimental import pallas as pl
from jax.experimental.pallas import tpu as pltpu
from jax.sharding import PartitionSpec as P

OFFSETS = (1, -1, 2, -2)
F32 = jnp.float32
BF16 = jnp.bfloat16
VMEM = pl.BlockSpec(memory_space=pltpu.VMEM)
SMEM = pl.BlockSpec(memory_space=pltpu.SMEM)
NB, BLK, C, MAXT, NSEND = 8, 256, 128, 24, 2
NEXT = NB + 4 * NSEND


ROUNDS = ("A", "C", "B", "D")


def partner_of(device, kind):
    if kind == "A":
        return device + 2 if device % 4 < 2 else device - 2
    if kind == "B":
        return device - 2 if device % 4 < 2 else device + 2
    if kind == "C":
        return device + 1 if device % 2 == 0 else device - 1
    return device - 1 if device % 2 == 0 else device + 1


def positions():
    me = lax.axis_index("sky")
    high = lax.rem(me, 4) // 2
    odd = lax.rem(me, 2)
    where = {"A": 2 + high, "B": 3 - high, "C": odd, "D": 1 - odd}
    return [where[kind] for kind in ROUNDS]


def opposite(position):
    return position + 1 - 2 * lax.rem(position, 2)


def mm(a, b):
    return jnp.dot(a, b, preferred_element_type=F32)


def call(kernel, name, outs, out_specs, in_specs, scratch, flops, args):
    size = sum(math.prod(o.shape) * o.dtype.itemsize for o in outs)
    size += sum(math.prod(a.shape) * a.dtype.itemsize for a in args)
    return pl.pallas_call(
        kernel,
        name=name,
        out_shape=outs,
        in_specs=in_specs,
        out_specs=out_specs,
        scratch_shapes=scratch,
        cost_estimate=pl.CostEstimate(flops=flops, bytes_accessed=size, transcendentals=0),
        compiler_params=pltpu.CompilerParams(vmem_limit_bytes=24 * 1024 * 1024),
    )(*args)


PIECE = jax.ShapeDtypeStruct((NSEND, BLK, C), BF16)
PIECE_T = jax.ShapeDtypeStruct((NSEND, C, BLK), BF16)
BLOCKS = jax.ShapeDtypeStruct((NB, BLK, C), BF16)
BLOCKS_T = jax.ShapeDtypeStruct((NB, C, BLK), BF16)
OWN_T = jax.ShapeDtypeStruct((NB, C, BLK), F32)
STEP_FLOPS = 2 * MAXT * BLK * BLK * C


def put_pieces(send, blocks, outs):
    for out, position in zip(outs, positions()):
        for j in range(NSEND):
            out[j] = blocks[send[0, position, j]]


def pick_kernel(send, blocks, *outs):
    put_pieces(send, blocks, outs)


def pick(send, blocks):
    return call(pick_kernel, "pick", [PIECE] * 4, [VMEM] * 4, [SMEM, VMEM], [], 0, (send, blocks))


def forward_kernel(first, last, *refs):
    refs = list(refs)
    take = lambda n: [refs.pop(0) for _ in range(n)]
    target, source, count, send, tiles, blocks = take(6)
    arrived = take(4)
    before = None if first else take(1)[0]
    if last:
        base, filters = take(2)
        (out,) = take(1)
    else:
        (out,) = take(1)
        pieces = take(4)
    ext, acc = take(2)
    ext[0:NB] = blocks[...]
    for piece, position in zip(arrived, positions()):
        for j in range(NSEND):
            ext[NB + opposite(position) * NSEND + j] = piece[j]
    acc[...] = jnp.zeros_like(acc)
    for t in range(MAXT):
        where = jnp.where(t < count[0], target[0, t], NB)
        acc[where] += mm(tiles[t], ext[source[0, t]])
    for b in range(NB):
        value = acc[b]
        if not first:
            value = 2.0 * value - before[b].astype(F32)
        value = value.astype(BF16)
        if last:
            result = mm(base[b], filters[0]) + mm(before[b], filters[1])
            result = result + mm(blocks[b], filters[2]) + mm(value, filters[3])
            out[b] = result.astype(BF16)
        else:
            out[b] = value
    if not last:
        put_pieces(send, out, pieces)


def forward(tables, send, tiles, blocks, arrived, before=None, base=None, filters=None):
    first, last = before is None, base is not None
    args = [*tables, send, tiles, blocks, *arrived]
    specs = [SMEM] * 4 + [VMEM] * 6
    if not first:
        args.append(before)
        specs.append(VMEM)
    if last:
        args += [base, filters]
        specs += [VMEM, VMEM]
        outs, out_specs = [BLOCKS], [VMEM]
    else:
        outs, out_specs = [BLOCKS] + [PIECE] * 4, [VMEM] * 5
    scratch = [pltpu.VMEM((NEXT, BLK, C), BF16), pltpu.VMEM((NB + 1, BLK, C), F32)]
    kernel = lambda *refs: forward_kernel(first, last, *refs)
    return call(kernel, "forward", outs, out_specs, specs, scratch, STEP_FLOPS, args)


def push_terms(target, source, count, tiles, held, acc, own, pieces):
    acc[...] = jnp.zeros_like(acc)
    for t in range(MAXT):
        where = jnp.where(t < count[0], source[0, t], NEXT)
        acc[where] += mm(held[target[0, t]], tiles[t])
    for piece, position in zip(pieces, positions()):
        for j in range(NSEND):
            piece[j] = acc[NB + opposite(position) * NSEND + j].astype(BF16)
    own[...] = acc[0:NB]


def adjoint_start_kernel(target, source, count, tiles, upstream, held, own, *rest):
    pieces = rest[:4]
    (acc,) = rest[4:]
    for b in range(NB):
        held[b] = upstream[b].astype(F32).T.astype(BF16)
    push_terms(target, source, count, tiles, held, acc, own, pieces)


ACC_T = pltpu.VMEM((NEXT + 1, C, BLK), F32)


def adjoint_start(tables, tiles, upstream):
    return call(
        adjoint_start_kernel, "adjoint_start", [BLOCKS_T, OWN_T] + [PIECE_T] * 4, [VMEM] * 6,
        [SMEM] * 3 + [VMEM, VMEM], [ACC_T], STEP_FLOPS, (*tables, tiles, upstream),
    )


def gather_terms(send, own, arrived, total):
    total[...] = own[...]
    for piece, position in zip(arrived, positions()):
        for j in range(NSEND):
            total[send[0, position, j]] += piece[j].astype(F32)


def adjoint_kernel(first, *refs):
    refs = list(refs)
    take = lambda n: [refs.pop(0) for _ in range(n)]
    target, source, count, send, tiles, own_in = take(6)
    arrived = take(4)
    before = None if first else take(1)[0]
    held, own = take(2)
    pieces = take(4)
    (acc,) = take(1)
    total = acc.at[pl.ds(0, NB)]
    gather_terms(send, own_in, arrived, total)
    for b in range(NB):
        value = total[b]
        if not first:
            value = 2.0 * value - before[b].astype(F32)
        held[b] = value.astype(BF16)
    push_terms(target, source, count, tiles, held, acc, own, pieces)


def adjoint(tables, send, tiles, own, arrived, before=None):
    first = before is None
    args = [*tables, send, tiles, own, *arrived] + ([] if first else [before])
    specs = [SMEM] * 4 + [VMEM] * (6 if first else 7)
    kernel = lambda *refs: adjoint_kernel(first, *refs)
    return call(
        kernel, "adjoint", [BLOCKS_T, OWN_T] + [PIECE_T] * 4, [VMEM] * 6, specs,
        [ACC_T], STEP_FLOPS, args,
    )


def adjoint_end_kernel(send, own_in, a0, a1, a2, a3, u0, u1, u2, filters, out, total):
    gather_terms(send, own_in, (a0, a1, a2, a3), total)
    for b in range(NB):
        u3 = (2.0 * total[b] - u1[b].astype(F32)).astype(BF16)
        grad = mm(filters[0], u0[b]) + mm(filters[1], u1[b])
        grad = grad + mm(filters[2], u2[b]) + mm(filters[3], u3)
        out[b] = grad.T.astype(BF16)


def adjoint_end(send, own, arrived, us, filters):
    return call(
        adjoint_end_kernel, "adjoint_end", [BLOCKS], [VMEM], [SMEM] + [VMEM] * 9,
        [pltpu.VMEM((NB, C, BLK), F32)], 8 * NB * BLK * C * C, (send, own, *arrived, *us, filters),
    )[0]


def grads_kernel(base, one, two, u0, u1, out):
    g0 = jnp.zeros((C, C), F32)
    g1, g2, g3 = g0, g0, g0
    for b in range(NB):
        g0 += mm(u0[b], base[b])
        g1 += mm(u0[b], one[b])
        g2 += mm(u0[b], two[b])
        g3 += mm(u1[b], two[b])
    out[0] = g0.T
    out[1] = g1.T
    out[2] = g2.T
    out[3] = (2.0 * g3 - g1).T


def grads(base, one, two, u0, u1):
    return call(
        grads_kernel, "grads", [jax.ShapeDtypeStruct((4, C, C), F32)], [VMEM], [VMEM] * 5, [],
        8 * NB * BLK * C * C, (base, one, two, u0, u1),
    )[0]


def spread(pieces):
    size = lax.axis_size("sky")
    got = []
    for piece, kind in zip(pieces, ROUNDS):
        pairs = [(i, partner_of(i, kind)) for i in range(size)]
        pairs = [(i, j) for i, j in pairs if 0 <= j < size]
        got.append(lax.ppermute(piece, "sky", pairs))
    return got


def total_over_devices(local):
    axes = ("view", "sky")
    count = lax.axis_size("view") * lax.axis_size("sky")
    rows = local.shape[0] * local.shape[1] // count
    parts = lax.all_to_all(local.reshape(count, rows, C), axes, 0, 0, tiled=True)
    part = jnp.sum(parts, axis=0)
    whole = lax.all_to_all(jnp.broadcast_to(part[None], parts.shape), axes, 0, 0, tiled=True)
    return whole.reshape(local.shape)


def per_device(
    pixels, cotangent, filters, lap_tiles, tile_target, tile_source, tile_count, send_blocks
):
    base = pixels.reshape(NB, BLK, C)
    upstream = cotangent.reshape(NB, BLK, C)
    tiles = lap_tiles.reshape(MAXT, BLK, BLK)
    tables = (tile_target, tile_source, tile_count)
    send = send_blocks

    f1 = spread(pick(send, base))
    u0, own, *terms = adjoint_start(tables, tiles, upstream)
    b1 = spread(terms)
    one, *pieces = forward(tables, send, tiles, base, f1)
    f2 = spread(pieces)
    u1, own, *terms = adjoint(tables, send, tiles, own, b1)
    b2 = spread(terms)
    two, *pieces = forward(tables, send, tiles, one, f2, before=base)
    local = grads(base, one, two, u0, u1)
    summed = total_over_devices(local)
    f3 = spread(pieces)
    u2, own, *terms = adjoint(tables, send, tiles, own, b2, before=u0)
    b3 = spread(terms)
    (outputs,) = forward(tables, send, tiles, two, f3, before=one, base=base, filters=filters)
    pixel_grad = adjoint_end(send, own, b3, (u0, u1, u2), filters)
    scale = 1.0 / math.sqrt(lax.axis_size("view") * lax.axis_size("sky") * NB * BLK)
    return (outputs.reshape(pixels.shape), pixel_grad.reshape(pixels.shape), summed * scale)


def solution(mesh):
    return jax.shard_map(
        per_device,
        mesh=mesh,
        in_specs=(
            P("view", "sky", None),
            P("view", "sky", None),
            P(),
            P("sky", None, None, None),
            P("sky", None),
            P("sky", None),
            P("sky"),
            P("sky", None, None),
        ),
        out_specs=(P("view", "sky", None), P("view", "sky", None), P()),
        check_vma=False,
    )
```

```python
import math

import jax
import jax.numpy as jnp
from jax import lax
from jax.experimental import pallas as pl
from jax.experimental.pallas import tpu as pltpu
from jax.sharding import PartitionSpec as P

OFFSETS = (1, -1, 2, -2)
F32 = jnp.float32
BF16 = jnp.bfloat16
VMEM = pl.BlockSpec(memory_space=pltpu.VMEM)
SMEM = pl.BlockSpec(memory_space=pltpu.SMEM)
HBM = pl.BlockSpec(memory_space=pltpu.HBM)
NB, BLK, C, MAXT, NSEND = 8, 256, 128, 24, 2
NEXT = NB + 4 * NSEND


ROUNDS = ("A", "C", "B", "D")


def partner_of(device, kind):
    if kind == "A":
        return device + 2 if device % 4 < 2 else device - 2
    if kind == "B":
        return device - 2 if device % 4 < 2 else device + 2
    if kind == "C":
        return device + 1 if device % 2 == 0 else device - 1
    return device - 1 if device % 2 == 0 else device + 1


def positions():
    me = lax.axis_index("sky")
    high = lax.rem(me, 4) // 2
    odd = lax.rem(me, 2)
    where = {"A": 2 + high, "B": 3 - high, "C": odd, "D": 1 - odd}
    return [where[kind] for kind in ROUNDS]


def opposite(position):
    return position + 1 - 2 * lax.rem(position, 2)


def mm(a, b):
    return jnp.dot(a, b, preferred_element_type=F32)


def call(kernel, name, outs, out_specs, in_specs, scratch, flops, args):
    size = sum(math.prod(o.shape) * o.dtype.itemsize for o in outs)
    size += sum(math.prod(a.shape) * a.dtype.itemsize for a in args)
    pin = pltpu.with_memory_space_constraint
    args = [pin(a, pltpu.HBM) if spec is HBM else a for a, spec in zip(args, in_specs)]
    outs = [pltpu.HBM(o.shape, o.dtype) if spec is HBM else o for o, spec in zip(outs, out_specs)]
    return pl.pallas_call(
        kernel,
        name=name,
        out_shape=outs,
        in_specs=in_specs,
        out_specs=out_specs,
        scratch_shapes=scratch,
        cost_estimate=pl.CostEstimate(flops=flops, bytes_accessed=size, transcendentals=0),
        compiler_params=pltpu.CompilerParams(vmem_limit_bytes=24 * 1024 * 1024),
    )(*args)


BLOCKS = jax.ShapeDtypeStruct((NB, BLK, C), BF16)
BLOCKS_T = jax.ShapeDtypeStruct((NB, C, BLK), BF16)
OWN_T = jax.ShapeDtypeStruct((NB, C, BLK), F32)
LETTER = jax.ShapeDtypeStruct((2 * NSEND, BLK, C), BF16)
GRADS = jax.ShapeDtypeStruct((4 * C, C), BF16)
ACC = pltpu.VMEM((NB + 1, BLK, C), F32)
ACC_T = pltpu.VMEM((NEXT + 1, C, BLK), F32)
EXT = pltpu.VMEM((NEXT, BLK, C), BF16)
STEP_FLOPS = 2 * MAXT * BLK * BLK * C


def put_blocks(send, blocks, letters):
    for letter, position in zip(letters, positions()):
        for j in range(NSEND):
            letter[j] = blocks[send[0, position, j]]


def put_terms(acc, letters):
    for letter, position in zip(letters, positions()):
        for j in range(NSEND):
            term = acc[NB + opposite(position) * NSEND + j].astype(BF16)
            letter[NSEND + j, 0:C] = term[:, 0:C]
            letter[NSEND + j, C:BLK] = term[:, C:BLK]


def apply_forward(target, source, count, tiles, blocks, letters, ext, acc):
    ext[0:NB] = blocks[...]
    for letter, position in zip(letters, positions()):
        for j in range(NSEND):
            ext[NB + opposite(position) * NSEND + j] = letter[j]
    acc[...] = jnp.zeros_like(acc)
    for t in range(MAXT):
        where = jnp.where(t < count[0], target[0, t], NB)
        acc[where] += mm(tiles[t], ext[source[0, t]])


def apply_transposed(target, source, count, tiles, held, acc, which=range(MAXT)):
    for t in which:
        where = jnp.where(t < count[0], source[0, t], NEXT)
        acc[where] += mm(held[target[0, t]], tiles[t])


def gather_terms(send, own, letters, total):
    total[...] = own[...]
    for letter, position in zip(letters, positions()):
        for j in range(NSEND):
            block = send[0, position, j]
            total[block, :, 0:C] += letter[NSEND + j, 0:C].astype(F32)
            total[block, :, C:BLK] += letter[NSEND + j, C:BLK].astype(F32)


TILE_GROUPS = 4


def start_kernel(count, target_in, source_in, send_in, tiles_in, base, upstream_in, u0, own, *rest):
    letters = rest[:4]
    target, source, send, tiles, upstream, acc, table_sem, map_sem, tile_sem, letter_sem = rest[4:]
    copy = pltpu.make_async_copy
    tables = [
        copy(send_in, send, table_sem.at[0]),
        copy(target_in, target, table_sem.at[1]),
        copy(source_in, source, table_sem.at[2]),
    ]
    for one in tables:
        one.start()
    map_copy = copy(upstream_in, upstream, map_sem)
    map_copy.start()
    size = MAXT // TILE_GROUPS
    tile_copies = []
    for g in range(TILE_GROUPS):
        part = pl.ds(g * size, size)
        tile_copies.append(copy(tiles_in.at[part], tiles.at[part], tile_sem.at[g]))
        tile_copies[g].start()
    acc[...] = jnp.zeros_like(acc)
    for one in tables:
        one.wait()
    block_copies = []
    for k, position in enumerate(positions()):
        for j in range(NSEND):
            block_copies.append(
                copy(base.at[send[0, position, j]], letters[k].at[j], letter_sem.at[k * NSEND + j])
            )
    for one in block_copies:
        one.start()
    map_copy.wait()
    for b in range(NB):
        u0[b] = upstream[b].astype(F32).T.astype(BF16)
    for g in range(TILE_GROUPS):
        tile_copies[g].wait()
        group = range(g * size, (g + 1) * size)
        apply_transposed(target, source, count, tiles, u0, acc, group)
    for one in block_copies:
        one.wait()
    put_terms(acc, letters)
    own[...] = acc[0:NB]


def start(tables, tiles, base, upstream):
    target, source, count, send = tables
    dma = pltpu.SemaphoreType.DMA
    scratch = [
        pltpu.SMEM(target.shape, jnp.int32),
        pltpu.SMEM(source.shape, jnp.int32),
        pltpu.SMEM(send.shape, jnp.int32),
        pltpu.VMEM(tiles.shape, BF16),
        pltpu.VMEM(upstream.shape, BF16),
        ACC_T,
        dma((3,)),
        dma,
        dma((TILE_GROUPS,)),
        dma((4 * NSEND,)),
    ]
    return call(
        start_kernel, "start", [BLOCKS_T, OWN_T] + [LETTER] * 4, [VMEM] * 6,
        [SMEM] + [HBM] * 6, scratch, STEP_FLOPS, (count, target, source, send, tiles, base, upstream),
    )


def advance(first, scale, ins, arrived, cheb_out, u_out, letters, grads, scratch, sent):
    target, source, count, send, tiles, cheb, own_in = ins[:7]
    ext, acc, acc_t = scratch
    apply_forward(target, source, count, tiles, cheb, arrived, ext, acc)
    if not first:
        u0, cheb_before, u_before = ins[7:]
    for b in range(NB):
        value = acc[b]
        if not first:
            value = 2.0 * value - cheb_before[b].astype(F32)
        cheb_out[b] = value.astype(BF16)
    put_blocks(send, cheb_out, letters)
    sent("forward")
    if not first:
        g0 = jnp.zeros((C, C), F32)
        g1, g2, g3 = g0, g0, g0
        for b in range(NB):
            g0 += mm(u0[b], cheb_before[b])
            g1 += mm(u0[b], cheb[b])
            g2 += mm(u0[b], cheb_out[b])
            g3 += mm(u_before[b], cheb_out[b])
        for k, grad in enumerate((g0, g1, g2, 2.0 * g3 - g1)):
            grads[k * C : (k + 1) * C] = (scale * grad.T).astype(BF16)
        sent("grads")
    gather_terms(send, own_in, arrived, acc_t.at[pl.ds(0, NB)])
    for b in range(NB):
        value = acc_t[b]
        if not first:
            value = 2.0 * value - u0[b].astype(F32)
        u_out[b] = value.astype(BF16)
    sent("adjoint")
    acc_t[...] = jnp.zeros_like(acc_t)
    apply_transposed(target, source, count, tiles, u_out, acc_t)
    put_terms(acc_t, letters)


def first_step_kernel(*refs):
    ins, arrived, outs = refs[:7], refs[7:11], refs[11:18]
    scratch = refs[18:]
    cheb_out, u_out, own = outs[:3]
    advance(True, None, ins, arrived, cheb_out, u_out, outs[3:], None, scratch, lambda what: None)
    own[...] = scratch[2][0:NB]


def first_step(tables, tiles, cheb, own, arrived):
    args = [*tables, tiles, cheb, own, *arrived]
    outs = [BLOCKS, BLOCKS_T, OWN_T] + [LETTER] * 4
    return call(
        first_step_kernel, "first_step", outs, [VMEM] * len(outs),
        [SMEM] * 4 + [VMEM] * (len(args) - 4), [EXT, ACC, ACC_T], 2 * STEP_FLOPS, args,
    )


def second_step_kernel(scale, *refs):
    ins, arrived, outs = refs[:10], refs[10:14], refs[14:22]
    scratch, (cheb_out, u_out, letters, grads, sem) = refs[22:25], refs[25:]
    letters = [letters.at[k] for k in range(4)]
    copies = []

    def send_off(here, there):
        copies.append(pltpu.make_async_copy(here, there, sem.at[len(copies)]))
        copies[-1].start()

    def sent(what):
        if what == "forward":
            send_off(cheb_out, outs[0])
        elif what == "grads":
            send_off(grads, outs[7])
        else:
            send_off(u_out, outs[1])

    advance(False, scale, ins, arrived, cheb_out, u_out, letters, grads, scratch, sent)
    for k in range(4):
        send_off(letters[k], outs[3 + k])
    send_off(scratch[2].at[pl.ds(0, NB)], outs[2])
    for copy in copies:
        copy.wait()


def second_step(tables, tiles, cheb, own, arrived, scale, u0, cheb_before, u_before):
    args = [*tables, tiles, cheb, own, u0, cheb_before, u_before, *arrived]
    outs = [BLOCKS, BLOCKS_T, OWN_T] + [LETTER] * 4 + [GRADS]
    scratch = [EXT, ACC, ACC_T]
    scratch += [pltpu.VMEM(o.shape, o.dtype) for o in (BLOCKS, BLOCKS_T)]
    scratch += [pltpu.VMEM((4, *LETTER.shape), BF16), pltpu.VMEM(GRADS.shape, BF16)]
    scratch += [pltpu.SemaphoreType.DMA((8,))]
    return call(
        lambda *refs: second_step_kernel(scale, *refs), "second_step", outs, [HBM] * len(outs),
        [SMEM] * 4 + [VMEM] * (len(args) - 4), scratch, 2 * STEP_FLOPS, args,
    )


def end_kernel(target, source, count, send, tiles, filters, *refs):
    sources, (out, grad_out), stages = refs[:11], refs[11:13], refs[13:24]
    sem, ext, acc, total = refs[24:]
    copies = [pltpu.make_async_copy(a, b, sem.at[k]) for k, (a, b) in enumerate(zip(sources, stages))]
    for copy in copies:
        copy.start()
    arrived, own, c2, u1, u2, u0, c1, c0 = stages[:4], *stages[4:]
    for copy in copies[:9]:
        copy.wait()
    gather_terms(send, own, arrived, total)
    for b in range(NB):
        u3 = (2.0 * total[b] - u1[b].astype(F32)).astype(BF16)
        grad = mm(filters[0], u0[b]) + mm(filters[1], u1[b])
        grad = grad + mm(filters[2], u2[b]) + mm(filters[3], u3)
        grad_out[b] = grad.T.astype(BF16)
    apply_forward(target, source, count, tiles, c2, arrived, ext, acc)
    for copy in copies[9:]:
        copy.wait()
    for b in range(NB):
        c3 = (2.0 * acc[b] - c1[b].astype(F32)).astype(BF16)
        result = mm(c0[b], filters[0]) + mm(c1[b], filters[1])
        result = result + mm(c2[b], filters[2]) + mm(c3, filters[3])
        out[b] = result.astype(BF16)


END_FLOPS = 30 * STEP_FLOPS


def end(tables, tiles, filters, chebs, us, own, arrived):
    (c0, c1, c2), (u0, u1, u2) = chebs, us
    sources = (*arrived, own, c2, u1, u2, u0, c1, c0)
    args = (*tables, tiles, filters, *sources)
    scratch = [pltpu.VMEM(a.shape, a.dtype) for a in sources]
    scratch += [pltpu.SemaphoreType.DMA((len(sources),))]
    scratch += [EXT, ACC, pltpu.VMEM((NB, C, BLK), F32)]
    return call(
        end_kernel, "end", [BLOCKS, BLOCKS], [VMEM] * 2,
        [SMEM] * 4 + [VMEM] * 2 + [HBM] * len(sources), scratch, END_FLOPS, args,
    )


def trade(letters):
    size = lax.axis_size("sky")
    got = []
    for letter, kind in zip(letters, ROUNDS):
        pairs = [(i, partner_of(i, kind)) for i in range(size)]
        pairs = [(i, j) for i, j in pairs if 0 <= j < size]
        got.append(lax.ppermute(letter, "sky", pairs))
    return got


def fold_kernel(parts, out):
    groups = parts.shape[0] // 16
    total = parts[0:16].astype(F32)
    for g in range(1, groups):
        total = total + parts[16 * g : 16 * (g + 1)].astype(F32)
    for shift in (8, 4, 2):
        total = total + pltpu.roll(total, shift, axis=0)
    for g in range(groups):
        out[16 * g : 16 * (g + 1)] = total.astype(BF16)


def total_over_devices(local):
    axes = ("view", "sky")
    count = lax.axis_size("view") * lax.axis_size("sky")
    assert local.shape[0] == 2 * count
    parts = lax.all_to_all(local.reshape(count, 2, C), axes, 0, 0, tiled=True)
    whole = call(
        fold_kernel, "fold", [GRADS], [VMEM], [VMEM], [], END_FLOPS, (parts.reshape(local.shape),)
    )[0]
    whole = lax.all_to_all(whole.reshape(count, 2, C), axes, 0, 0, tiled=True)
    return whole.reshape(4, C, C).astype(F32)


def per_device(
    pixels, cotangent, filters, lap_tiles, tile_target, tile_source, tile_count, send_blocks
):
    c0 = pixels.reshape(NB, BLK, C)
    upstream = cotangent.reshape(NB, BLK, C)
    tiles = lap_tiles.reshape(MAXT, BLK, BLK)
    tables = (tile_target, tile_source, tile_count, send_blocks)
    scale = 1.0 / math.sqrt(lax.axis_size("view") * lax.axis_size("sky") * NB * BLK)

    u0, own, *letters = start(tables, tiles, c0, upstream)
    arrived = trade(letters)
    c1, u1, own, *letters = first_step(tables, tiles, c0, own, arrived)
    arrived = trade(letters)
    c2, u2, own, *letters, local = second_step(tables, tiles, c1, own, arrived, scale, u0, c0, u1)
    filter_grad = total_over_devices(local)
    arrived = trade(letters)
    outputs, pixel_grad = end(tables, tiles, filters, (c0, c1, c2), (u0, u1, u2), own, arrived)
    return (outputs.reshape(pixels.shape), pixel_grad.reshape(pixels.shape), filter_grad)


def solution(mesh):
    return jax.shard_map(
        per_device,
        mesh=mesh,
        in_specs=(
            P("view", "sky", None),
            P("view", "sky", None),
            P(),
            P("sky", None, None, None),
            P("sky", None),
            P("sky", None),
            P("sky"),
            P("sky", None, None),
        ),
        out_specs=(P("view", "sky", None), P("view", "sky", None), P()),
        check_vma=False,
    )
```

```python
import math

import jax
import jax.numpy as jnp
from jax import lax
from jax.experimental import pallas as pl
from jax.experimental.pallas import tpu as pltpu
from jax.sharding import Mesh
from jax.sharding import PartitionSpec as P

OFFSETS = (1, -1, 2, -2)
F32 = jnp.float32
BF16 = jnp.bfloat16
VMEM = pl.BlockSpec(memory_space=pltpu.VMEM)
SMEM = pl.BlockSpec(memory_space=pltpu.SMEM)
HBM = pl.BlockSpec(memory_space=pltpu.HBM)
NB, BLK, C, MAXT, NSEND = 8, 256, 128, 24, 2
NEXT = NB + 4 * NSEND
PLANE = 16
SKY = ("z", "plane")


ROUNDS = ("A", "C", "D", "B")


def partner_of(device, kind):
    if kind == "A":
        return device + 2 if device % 4 < 2 else device - 2
    if kind == "B":
        return device - 2 if device % 4 < 2 else device + 2
    if kind == "C":
        return device + 1 if device % 2 == 0 else device - 1
    return device - 1 if device % 2 == 0 else device + 1


def positions():
    me = lax.axis_index(SKY)
    high = lax.rem(me, 4) // 2
    odd = lax.rem(me, 2)
    where = {"A": 2 + high, "B": 3 - high, "C": odd, "D": 1 - odd}
    return [where[kind] for kind in ROUNDS]


def opposite(position):
    return position + 1 - 2 * lax.rem(position, 2)


def mm(a, b):
    return jnp.dot(a, b, preferred_element_type=F32)


def call(kernel, name, outs, out_specs, in_specs, scratch, flops, args):
    size = sum(math.prod(o.shape) * o.dtype.itemsize for o in outs)
    size += sum(math.prod(a.shape) * a.dtype.itemsize for a in args)
    pin = pltpu.with_memory_space_constraint
    args = [pin(a, pltpu.HBM) if spec is HBM else a for a, spec in zip(args, in_specs)]
    outs = [pltpu.HBM(o.shape, o.dtype) if spec is HBM else o for o, spec in zip(outs, out_specs)]
    return pl.pallas_call(
        kernel,
        name=name,
        out_shape=outs,
        in_specs=in_specs,
        out_specs=out_specs,
        scratch_shapes=scratch,
        cost_estimate=pl.CostEstimate(flops=flops, bytes_accessed=size, transcendentals=0),
        compiler_params=pltpu.CompilerParams(vmem_limit_bytes=24 * 1024 * 1024),
    )(*args)


BLOCKS = jax.ShapeDtypeStruct((NB, BLK, C), BF16)
BLOCKS_T = jax.ShapeDtypeStruct((NB, C, BLK), BF16)
OWN_T = jax.ShapeDtypeStruct((NB, C, BLK), F32)
MAPS, TERMS = pl.ds(0, NSEND), pl.ds(NSEND, NSEND)
LETTER = jax.ShapeDtypeStruct((2 * NSEND, BLK, C), BF16)
GRADS = jax.ShapeDtypeStruct((4 * C, C), BF16)
ACC = pltpu.VMEM((NB + 1, BLK, C), F32)
ACC_T = pltpu.VMEM((NEXT + 1, C, BLK), F32)
EXT = pltpu.VMEM((NEXT, BLK, C), BF16)
STEP_FLOPS = 2 * MAXT * BLK * BLK * C


def turned(block):
    rows = lax.broadcasted_iota(jnp.int32, (C, C), 0)
    unit = (rows == lax.broadcasted_iota(jnp.int32, (C, C), 1)).astype(BF16)
    product = lax.dot_general(unit, block, (((1,), (1,)), ((), ())), preferred_element_type=F32)
    return product.astype(BF16)


def put_blocks(send, blocks, letters):
    for letter, position in zip(letters, positions()):
        for j in range(NSEND):
            letter[j] = blocks[send[0, j, position]]


def put_terms(acc, letters):
    for letter, position in zip(letters, positions()):
        for j in range(NSEND):
            term = acc[NB + opposite(position) * NSEND + j].astype(BF16)
            letter[NSEND + j, 0:C] = term[:, 0:C]
            letter[NSEND + j, C:BLK] = term[:, C:BLK]


def apply_forward(target, source, count, tiles, blocks, letters, ext, acc):
    ext[0:NB] = blocks[...]
    for letter, position in zip(letters, positions()):
        for j in range(NSEND):
            ext[NB + opposite(position) * NSEND + j] = letter[j]
    acc[...] = jnp.zeros_like(acc)
    for t in range(MAXT):
        where = jnp.where(t < count[0], target[0, t], NB)
        acc[where] += mm(tiles[t], ext[source[0, t]])


def apply_transposed(target, source, count, tiles, held, acc, which=range(MAXT)):
    for t in which:
        where = jnp.where(t < count[0], source[0, t], NEXT)
        acc[where] += mm(held[target[0, t]], tiles[t])


def gather_terms(send, own, letters, total):
    total[...] = own[...]
    for letter, position in zip(letters, positions()):
        for j in range(NSEND):
            block = send[0, j, position]
            total[block, :, 0:C] += letter[NSEND + j, 0:C].astype(F32)
            total[block, :, C:BLK] += letter[NSEND + j, C:BLK].astype(F32)


TILE_GROUPS = 4


def start_kernel(count, target_in, source_in, send_in, tiles_in, base, upstream_in, u0, own, *rest):
    letters = rest[:4]
    target, source, send, tiles, upstream, acc, table_sem, map_sem, tile_sem, letter_sem = rest[4:]
    copy = pltpu.make_async_copy
    tables = [
        copy(send_in, send, table_sem.at[0]),
        copy(target_in, target, table_sem.at[1]),
        copy(source_in, source, table_sem.at[2]),
    ]
    for one in tables:
        one.start()
    map_copy = copy(upstream_in, upstream, map_sem)
    map_copy.start()
    size = MAXT // TILE_GROUPS
    tile_copies = []
    for g in range(TILE_GROUPS):
        part = pl.ds(g * size, size)
        tile_copies.append(copy(tiles_in.at[part], tiles.at[part], tile_sem.at[g]))
        tile_copies[g].start()
    acc[...] = jnp.zeros_like(acc)
    for one in tables:
        one.wait()
    block_copies = []
    for k, position in enumerate(positions()):
        for j in range(NSEND):
            block_copies.append(
                copy(base.at[send[0, j, position]], letters[k].at[j], letter_sem.at[k * NSEND + j])
            )
    for one in block_copies:
        one.start()
    map_copy.wait()
    for b in range(NB):
        u0[b] = turned(upstream[b])
    for g in range(TILE_GROUPS):
        tile_copies[g].wait()
        group = range(g * size, (g + 1) * size)
        apply_transposed(target, source, count, tiles, u0, acc, group)
    for one in block_copies:
        one.wait()
    put_terms(acc, letters)
    own[...] = acc[0:NB]


def start(tables, tiles, base, upstream):
    target, source, count, send = tables
    dma = pltpu.SemaphoreType.DMA
    scratch = [
        pltpu.SMEM(target.shape, jnp.int32),
        pltpu.SMEM(source.shape, jnp.int32),
        pltpu.SMEM(send.shape, jnp.int32),
        pltpu.VMEM(tiles.shape, BF16),
        pltpu.VMEM(upstream.shape, BF16),
        ACC_T,
        dma((3,)),
        dma,
        dma((TILE_GROUPS,)),
        dma((4 * NSEND,)),
    ]
    return call(
        start_kernel, "start", [BLOCKS_T, OWN_T] + [LETTER] * 4, [VMEM] * 6,
        [SMEM] + [HBM] * 6, scratch, STEP_FLOPS, (count, target, source, send, tiles, base, upstream),
    )


def advance(first, scale, ins, arrived, cheb_out, u_out, letters, grads, scratch, sent):
    target, source, count, send, tiles, cheb, own_in = ins[:7]
    ext, acc, acc_t = scratch
    if not first:
        u0, cheb_before, u_before = ins[7:]

    def adjoint_part():
        gather_terms(send, own_in, arrived, acc_t.at[pl.ds(0, NB)])
        for b in range(NB):
            value = acc_t[b]
            if not first:
                value = 2.0 * value - u0[b].astype(F32)
            u_out[b] = value.astype(BF16)
        sent("adjoint")
        acc_t[...] = jnp.zeros_like(acc_t)
        apply_transposed(target, source, count, tiles, u_out, acc_t)
        put_terms(acc_t, letters)
        sent("terms")

    def forward_part():
        apply_forward(target, source, count, tiles, cheb, arrived, ext, acc)
        for b in range(NB):
            value = acc[b]
            if not first:
                value = 2.0 * value - cheb_before[b].astype(F32)
            cheb_out[b] = value.astype(BF16)
        put_blocks(send, cheb_out, letters)
        sent("forward")

    for part in (forward_part, adjoint_part) if first else (adjoint_part, forward_part):
        part()
    if not first:
        g0 = jnp.zeros((C, C), F32)
        g1, g2, g3 = g0, g0, g0
        for b in range(NB):
            g0 += mm(u0[b], cheb_before[b])
            g1 += mm(u0[b], cheb[b])
            g2 += mm(u0[b], cheb_out[b])
            g3 += mm(u_before[b], cheb_out[b])
        for k, grad in enumerate((g0, g1, g2, 2.0 * g3 - g1)):
            grads[k * C : (k + 1) * C] = (scale * grad.T).astype(BF16)
        sent("grads")


def first_step_kernel(*refs):
    ins, arrived, outs = refs[:7], refs[7:11], refs[11:18]
    scratch = refs[18:]
    cheb_out, u_out, own = outs[:3]
    advance(True, None, ins, arrived, cheb_out, u_out, outs[3:], None, scratch, lambda what: None)
    own[...] = scratch[2][0:NB]


def first_step(tables, tiles, cheb, own, arrived):
    args = [*tables, tiles, cheb, own, *arrived]
    outs = [BLOCKS, BLOCKS_T, OWN_T] + [LETTER] * 4
    return call(
        first_step_kernel, "first_step", outs, [VMEM] * len(outs),
        [SMEM] * 4 + [VMEM] * (len(args) - 4), [EXT, ACC, ACC_T], 2 * STEP_FLOPS, args,
    )


def second_step_kernel(scale, *refs):
    ins, arrived, outs = refs[:10], refs[10:14], refs[14:22]
    scratch, (cheb_out, u_out, letters, grads, sem) = refs[22:25], refs[25:]
    letters = [letters.at[k] for k in range(4)]
    copies = []

    def send_off(here, there):
        copies.append(pltpu.make_async_copy(here, there, sem.at[len(copies)]))
        copies[-1].start()

    def sent(what):
        if what == "adjoint":
            send_off(u_out, outs[1])
        elif what == "terms":
            send_off(scratch[2].at[pl.ds(0, NB)], outs[2])
            for k in range(4):
                send_off(letters[k].at[TERMS], outs[3 + k].at[TERMS])
        elif what == "forward":
            send_off(cheb_out, outs[0])
            for k in range(4):
                send_off(letters[k].at[MAPS], outs[3 + k].at[MAPS])
        else:
            send_off(grads, outs[7])

    advance(False, scale, ins, arrived, cheb_out, u_out, letters, grads, scratch, sent)
    for copy in copies:
        copy.wait()


def second_step(tables, tiles, cheb, own, arrived, scale, u0, cheb_before, u_before):
    args = [*tables, tiles, cheb, own, u0, cheb_before, u_before, *arrived]
    outs = [BLOCKS, BLOCKS_T, OWN_T] + [LETTER] * 4 + [GRADS]
    scratch = [EXT, ACC, ACC_T]
    scratch += [pltpu.VMEM(o.shape, o.dtype) for o in (BLOCKS, BLOCKS_T)]
    scratch += [pltpu.VMEM((4, *LETTER.shape), BF16), pltpu.VMEM(GRADS.shape, BF16)]
    scratch += [pltpu.SemaphoreType.DMA((12,))]
    return call(
        lambda *refs: second_step_kernel(scale, *refs), "second_step", outs, [HBM] * len(outs),
        [SMEM] * 4 + [VMEM] * (len(args) - 4), scratch, 2 * STEP_FLOPS, args,
    )


def end_kernel(target, source, count, send, tiles, filters, *refs):
    sources, outs, stages = refs[:11], refs[11:13], refs[13:24]
    sem, ext, acc, total, ready, out_sem = refs[24:]
    copies = [pltpu.make_async_copy(a, b, sem.at[k]) for k, (a, b) in enumerate(zip(sources, stages))]
    for copy in copies:
        copy.start()
    arrived, c2, c1, c0, own, u1, u2, u0 = stages[:4], *stages[4:]
    written = []

    def write(which, b):
        half = NB // 2
        if (b + 1) % half == 0:
            part = pl.ds(b + 1 - half, half)
            k = len(written)
            written.append(
                pltpu.make_async_copy(ready.at[which, part], outs[which].at[part], out_sem.at[k])
            )
            written[k].start()

    for copy in copies[:5]:
        copy.wait()
    apply_forward(target, source, count, tiles, c2, arrived, ext, acc)
    for copy in copies[5:]:
        copy.wait()
    for b in range(NB):
        c3 = (2.0 * acc[b] - c1[b].astype(F32)).astype(BF16)
        result = mm(c0[b], filters[0]) + mm(c1[b], filters[1])
        result = result + mm(c2[b], filters[2]) + mm(c3, filters[3])
        ready[0, b] = result.astype(BF16)
        write(0, b)
    gather_terms(send, own, arrived, total)
    for b in range(NB):
        u3 = (2.0 * total[b] - u1[b].astype(F32)).astype(BF16)
        grad = mm(filters[0], u0[b]) + mm(filters[1], u1[b])
        grad = grad + mm(filters[2], u2[b]) + mm(filters[3], u3)
        ready[1, b] = grad.T.astype(BF16)
        write(1, b)
    for copy in written:
        copy.wait()


END_FLOPS = 30 * STEP_FLOPS


def end(tables, tiles, filters, chebs, us, own, arrived):
    (c0, c1, c2), (u0, u1, u2) = chebs, us
    sources = (*arrived, c2, c1, c0, own, u1, u2, u0)
    args = (*tables, tiles, filters, *sources)
    scratch = [pltpu.VMEM(a.shape, a.dtype) for a in sources]
    scratch += [pltpu.SemaphoreType.DMA((len(sources),))]
    scratch += [EXT, ACC, pltpu.VMEM((NB, C, BLK), F32)]
    scratch += [pltpu.VMEM((2, *BLOCKS.shape), BF16), pltpu.SemaphoreType.DMA((4,))]
    return call(
        end_kernel, "end", [BLOCKS, BLOCKS], [HBM] * 2,
        [SMEM] * 4 + [VMEM] * 2 + [HBM] * len(sources), scratch, END_FLOPS, args,
    )


def trade(letters):
    size = lax.axis_size(SKY)
    got = []
    for letter, kind in zip(letters, ROUNDS):
        pairs = [(i, partner_of(i, kind)) for i in range(size)]
        pairs = [(i, j) for i, j in pairs if 0 <= j < size]
        got.append(lax.ppermute(letter, SKY, pairs))
    return got


def fold_kernel(parts, out):
    members, rows = parts.shape[0], parts.shape[1]
    total = parts[0].astype(F32)
    for k in range(1, members):
        total = total + parts[k].astype(F32)
    total = total.astype(BF16)
    for k in range(members):
        out[k] = total


def total_over_devices(local):
    others = lax.axis_size("view") * lax.axis_size("z")
    rows = local.shape[0] // PLANE
    assert others == PLANE and rows % 16 == 0
    parts = local.reshape(PLANE, rows, C)
    for axes, flops in ((("plane",), END_FLOPS), (("view", "z"), 0)):
        parts = lax.all_to_all(parts, axes, 0, 0, tiled=True)
        shape = jax.ShapeDtypeStruct(parts.shape, BF16)
        parts = call(fold_kernel, "fold", [shape], [VMEM], [VMEM], [], flops, (parts,))[0]
    whole = lax.all_to_all(parts, ("plane",), 0, 0, tiled=True)
    return whole.reshape(4, C, C).astype(F32)


def per_device(
    pixels, cotangent, filters, lap_tiles, tile_target, tile_source, tile_count, send_blocks
):
    c0 = pixels.reshape(NB, BLK, C)
    upstream = cotangent.reshape(NB, BLK, C)
    tiles = lap_tiles.reshape(MAXT, BLK, BLK)
    tables = (tile_target, tile_source, tile_count, send_blocks.swapaxes(1, 2))
    scale = 1.0 / math.sqrt(lax.axis_size("view") * lax.axis_size(SKY) * NB * BLK)

    u0, own, *letters = start(tables, tiles, c0, upstream)
    arrived = trade(letters)
    c1, u1, own, *letters = first_step(tables, tiles, c0, own, arrived)
    arrived = trade(letters)
    c2, u2, own, *letters, local = second_step(tables, tiles, c1, own, arrived, scale, u0, c0, u1)
    filter_grad = total_over_devices(local)
    arrived = trade(letters)
    outputs, pixel_grad = end(tables, tiles, filters, (c0, c1, c2), (u0, u1, u2), own, arrived)
    return (outputs.reshape(pixels.shape), pixel_grad.reshape(pixels.shape), filter_grad)


def solution(mesh):
    views, skies = mesh.devices.shape
    fine = Mesh(mesh.devices.reshape(views, skies // PLANE, PLANE), ("view", *SKY))
    return jax.shard_map(
        per_device,
        mesh=fine,
        in_specs=(
            P("view", SKY, None),
            P("view", SKY, None),
            P(),
            P(SKY, None, None, None),
            P(SKY, None),
            P(SKY, None),
            P(SKY),
            P(SKY, None, None),
        ),
        out_specs=(P("view", SKY, None), P("view", SKY, None), P()),
        check_vma=False,
    )
```

```python
import math

import jax
import jax.numpy as jnp
from jax import lax
from jax.experimental import pallas as pl
from jax.experimental.pallas import tpu as pltpu
from jax.sharding import Mesh
from jax.sharding import PartitionSpec as P

OFFSETS = (1, -1, 2, -2)
F32 = jnp.float32
BF16 = jnp.bfloat16
VMEM = pl.BlockSpec(memory_space=pltpu.VMEM)
SMEM = pl.BlockSpec(memory_space=pltpu.SMEM)
HBM = pl.BlockSpec(memory_space=pltpu.HBM)
NB, BLK, C, MAXT, NSEND = 8, 256, 128, 24, 2
NEXT = NB + 4 * NSEND
PLANE = 16
SKY = ("z", "plane")


ROUNDS = ("A", "C", "D", "B")


def partner_of(device, kind):
    if kind == "A":
        return device + 2 if device % 4 < 2 else device - 2
    if kind == "B":
        return device - 2 if device % 4 < 2 else device + 2
    if kind == "C":
        return device + 1 if device % 2 == 0 else device - 1
    return device - 1 if device % 2 == 0 else device + 1


def positions():
    me = lax.axis_index(SKY)
    high = lax.rem(me, 4) // 2
    odd = lax.rem(me, 2)
    where = {"A": 2 + high, "B": 3 - high, "C": odd, "D": 1 - odd}
    return [where[kind] for kind in ROUNDS]


def opposite(position):
    return position + 1 - 2 * lax.rem(position, 2)


def mm(a, b):
    return jnp.dot(a, b, preferred_element_type=F32)


def call(kernel, name, outs, out_specs, in_specs, scratch, flops, args):
    size = sum(math.prod(o.shape) * o.dtype.itemsize for o in outs)
    size += sum(math.prod(a.shape) * a.dtype.itemsize for a in args)
    pin = pltpu.with_memory_space_constraint
    args = [pin(a, pltpu.HBM) if spec is HBM else a for a, spec in zip(args, in_specs)]
    outs = [pltpu.HBM(o.shape, o.dtype) if spec is HBM else o for o, spec in zip(outs, out_specs)]
    return pl.pallas_call(
        kernel,
        name=name,
        out_shape=outs,
        in_specs=in_specs,
        out_specs=out_specs,
        scratch_shapes=scratch,
        cost_estimate=pl.CostEstimate(flops=flops, bytes_accessed=size, transcendentals=0),
        compiler_params=pltpu.CompilerParams(vmem_limit_bytes=24 * 1024 * 1024),
    )(*args)


BLOCKS = jax.ShapeDtypeStruct((NB, BLK, C), BF16)
BLOCKS_T = jax.ShapeDtypeStruct((NB, C, BLK), BF16)
OWN_T = jax.ShapeDtypeStruct((NB, C, BLK), F32)
MAPS, TERMS = pl.ds(0, NSEND), pl.ds(NSEND, NSEND)
LETTER = jax.ShapeDtypeStruct((2 * NSEND, BLK, C), BF16)
GRADS = jax.ShapeDtypeStruct((4 * C, C), BF16)
ACC = pltpu.VMEM((NB + 1, BLK, C), F32)
ACC_T = pltpu.VMEM((NEXT + 1, C, BLK), F32)
EXT = pltpu.VMEM((NEXT, BLK, C), BF16)
STEP_FLOPS = 2 * MAXT * BLK * BLK * C


def turned(block):
    rows = lax.broadcasted_iota(jnp.int32, (C, C), 0)
    unit = (rows == lax.broadcasted_iota(jnp.int32, (C, C), 1)).astype(BF16)
    product = lax.dot_general(unit, block, (((1,), (1,)), ((), ())), preferred_element_type=F32)
    return product.astype(BF16)


def put_blocks(send, blocks, letters):
    for letter, position in zip(letters, positions()):
        for j in range(NSEND):
            letter[j] = blocks[send[0, j, position]]


def put_terms(acc, letters):
    for letter, position in zip(letters, positions()):
        for j in range(NSEND):
            term = acc[NB + opposite(position) * NSEND + j].astype(BF16)
            letter[NSEND + j, 0:C] = term[:, 0:C]
            letter[NSEND + j, C:BLK] = term[:, C:BLK]


def apply_forward(target, source, count, tiles, blocks, letters, ext, acc):
    ext[0:NB] = blocks[...]
    for letter, position in zip(letters, positions()):
        for j in range(NSEND):
            ext[NB + opposite(position) * NSEND + j] = letter[j]
    acc[...] = jnp.zeros_like(acc)
    for t in range(MAXT):
        where = jnp.where(t < count[0], target[0, t], NB)
        acc[where] += mm(tiles[t], ext[source[0, t]])


def apply_transposed(target, source, count, tiles, held, acc, which=range(MAXT)):
    for t in which:
        where = jnp.where(t < count[0], source[0, t], NEXT)
        acc[where] += mm(held[target[0, t]], tiles[t])


def gather_terms(send, own, letters, total):
    total[...] = own[...]
    for letter, position in zip(letters, positions()):
        for j in range(NSEND):
            block = send[0, j, position]
            total[block, :, 0:C] += letter[NSEND + j, 0:C].astype(F32)
            total[block, :, C:BLK] += letter[NSEND + j, C:BLK].astype(F32)


TILE_GROUPS = 4


def start_kernel(count, target_in, source_in, send_in, tiles_in, base, upstream_in, u0, own, tiles, *rest):
    letters = rest[:4]
    target, source, send, upstream, acc, table_sem, map_sem, tile_sem, letter_sem = rest[4:]
    copy = pltpu.make_async_copy
    tables = [
        copy(send_in, send, table_sem.at[0]),
        copy(target_in, target, table_sem.at[1]),
        copy(source_in, source, table_sem.at[2]),
    ]
    for one in tables:
        one.start()
    map_copy = copy(upstream_in, upstream, map_sem)
    map_copy.start()
    size = MAXT // TILE_GROUPS
    tile_copies = []
    for g in range(TILE_GROUPS):
        part = pl.ds(g * size, size)
        tile_copies.append(copy(tiles_in.at[part], tiles.at[part], tile_sem.at[g]))
        tile_copies[g].start()
    acc[...] = jnp.zeros_like(acc)
    for one in tables:
        one.wait()
    block_copies = []
    for k, position in enumerate(positions()):
        for j in range(NSEND):
            block_copies.append(
                copy(base.at[send[0, j, position]], letters[k].at[j], letter_sem.at[k * NSEND + j])
            )
    for one in block_copies:
        one.start()
    map_copy.wait()
    for b in range(NB):
        u0[b] = turned(upstream[b])
    for g in range(TILE_GROUPS):
        tile_copies[g].wait()
        group = range(g * size, (g + 1) * size)
        apply_transposed(target, source, count, tiles, u0, acc, group)
    for one in block_copies:
        one.wait()
    put_terms(acc, letters)
    own[...] = acc[0:NB]


def start(tables, tiles, base, upstream):
    target, source, count, send = tables
    dma = pltpu.SemaphoreType.DMA
    scratch = [
        pltpu.SMEM(target.shape, jnp.int32),
        pltpu.SMEM(source.shape, jnp.int32),
        pltpu.SMEM(send.shape, jnp.int32),
        pltpu.VMEM(upstream.shape, BF16),
        ACC_T,
        dma((3,)),
        dma,
        dma((TILE_GROUPS,)),
        dma((4 * NSEND,)),
    ]
    return call(
        start_kernel, "start", [BLOCKS_T, OWN_T, tiles] + [LETTER] * 4, [VMEM] * 7,
        [SMEM] + [HBM] * 6, scratch, STEP_FLOPS, (count, target, source, send, tiles, base, upstream),
    )


def advance(first, scale, ins, arrived, cheb_out, u_out, letters, grads, scratch, sent):
    target, source, count, send, tiles, cheb, own_in = ins[:7]
    ext, acc, acc_t = scratch
    if not first:
        u0, cheb_before, u_before = ins[7:]

    def adjoint_part():
        gather_terms(send, own_in, arrived, acc_t.at[pl.ds(0, NB)])
        for b in range(NB):
            value = acc_t[b]
            if not first:
                value = 2.0 * value - u0[b].astype(F32)
            u_out[b] = value.astype(BF16)
        sent("adjoint")
        acc_t[...] = jnp.zeros_like(acc_t)
        apply_transposed(target, source, count, tiles, u_out, acc_t)
        put_terms(acc_t, letters)
        sent("terms")

    def forward_part():
        apply_forward(target, source, count, tiles, cheb, arrived, ext, acc)
        for b in range(NB):
            value = acc[b]
            if not first:
                value = 2.0 * value - cheb_before[b].astype(F32)
            cheb_out[b] = value.astype(BF16)
        put_blocks(send, cheb_out, letters)
        sent("forward")

    for part in (forward_part, adjoint_part) if first else (adjoint_part, forward_part):
        part()
    if not first:
        g0 = jnp.zeros((C, C), F32)
        g1, g2, g3 = g0, g0, g0
        for b in range(NB):
            g0 += mm(u0[b], cheb_before[b])
            g1 += mm(u0[b], cheb[b])
            g2 += mm(u0[b], cheb_out[b])
            g3 += mm(u_before[b], cheb_out[b])
        for k, grad in enumerate((g0, g1, g2, 2.0 * g3 - g1)):
            grads[k * C : (k + 1) * C] = (scale * grad.T).astype(BF16)
        sent("grads")


def first_step_kernel(*refs):
    ins, arrived, outs = refs[:7], refs[7:11], refs[11:18]
    scratch = refs[18:]
    cheb_out, u_out, own = outs[:3]
    advance(True, None, ins, arrived, cheb_out, u_out, outs[3:], None, scratch, lambda what: None)
    own[...] = scratch[2][0:NB]


def first_step(tables, tiles, cheb, own, arrived):
    args = [*tables, tiles, cheb, own, *arrived]
    outs = [BLOCKS, BLOCKS_T, OWN_T] + [LETTER] * 4
    return call(
        first_step_kernel, "first_step", outs, [VMEM] * len(outs),
        [SMEM] * 4 + [VMEM] * (len(args) - 4), [EXT, ACC, ACC_T], 2 * STEP_FLOPS, args,
    )


def second_step_kernel(scale, *refs):
    ins, arrived, outs = refs[:10], refs[10:14], refs[14:22]
    scratch, (cheb_out, u_out, letters, grads, sem) = refs[22:25], refs[25:]
    letters = [letters.at[k] for k in range(4)]
    copies = []

    def send_off(here, there):
        copies.append(pltpu.make_async_copy(here, there, sem.at[len(copies)]))
        copies[-1].start()

    def sent(what):
        if what == "adjoint":
            send_off(u_out, outs[1])
        elif what == "terms":
            send_off(scratch[2].at[pl.ds(0, NB)], outs[2])
            for k in range(4):
                send_off(letters[k].at[TERMS], outs[3 + k].at[TERMS])
        elif what == "forward":
            send_off(cheb_out, outs[0])
            for k in range(4):
                send_off(letters[k].at[MAPS], outs[3 + k].at[MAPS])
        else:
            send_off(grads, outs[7])

    advance(False, scale, ins, arrived, cheb_out, u_out, letters, grads, scratch, sent)
    for copy in copies:
        copy.wait()


def second_step(tables, tiles, cheb, own, arrived, scale, u0, cheb_before, u_before):
    args = [*tables, tiles, cheb, own, u0, cheb_before, u_before, *arrived]
    outs = [BLOCKS, BLOCKS_T, OWN_T] + [LETTER] * 4 + [GRADS]
    scratch = [EXT, ACC, ACC_T]
    scratch += [pltpu.VMEM(o.shape, o.dtype) for o in (BLOCKS, BLOCKS_T)]
    scratch += [pltpu.VMEM((4, *LETTER.shape), BF16), pltpu.VMEM(GRADS.shape, BF16)]
    scratch += [pltpu.SemaphoreType.DMA((12,))]
    return call(
        lambda *refs: second_step_kernel(scale, *refs), "second_step", outs, [HBM] * len(outs),
        [SMEM] * 4 + [VMEM] * (len(args) - 4), scratch, 2 * STEP_FLOPS, args,
    )


def end_kernel(target, source, count, send, tiles, filters, *refs):
    sources, outs, stages = refs[:11], refs[11:13], refs[13:24]
    sem, ext, acc, total, ready, out_sem = refs[24:]
    copies = [pltpu.make_async_copy(a, b, sem.at[k]) for k, (a, b) in enumerate(zip(sources, stages))]
    for copy in copies:
        copy.start()
    arrived, c2, c1, c0, own, u1, u2, u0 = stages[:4], *stages[4:]
    written = []

    def write(which, b):
        half = NB // 2
        if (b + 1) % half == 0:
            part = pl.ds(b + 1 - half, half)
            k = len(written)
            written.append(
                pltpu.make_async_copy(ready.at[which, part], outs[which].at[part], out_sem.at[k])
            )
            written[k].start()

    for copy in copies[:5]:
        copy.wait()
    apply_forward(target, source, count, tiles, c2, arrived, ext, acc)
    for copy in copies[5:]:
        copy.wait()
    for b in range(NB):
        c3 = (2.0 * acc[b] - c1[b].astype(F32)).astype(BF16)
        result = mm(c0[b], filters[0]) + mm(c1[b], filters[1])
        result = result + mm(c2[b], filters[2]) + mm(c3, filters[3])
        ready[0, b] = result.astype(BF16)
        write(0, b)
    gather_terms(send, own, arrived, total)
    for b in range(NB):
        u3 = (2.0 * total[b] - u1[b].astype(F32)).astype(BF16)
        grad = mm(filters[0], u0[b]) + mm(filters[1], u1[b])
        grad = grad + mm(filters[2], u2[b]) + mm(filters[3], u3)
        ready[1, b] = grad.T.astype(BF16)
        write(1, b)
    for copy in written:
        copy.wait()


END_FLOPS = 30 * STEP_FLOPS


def end(tables, tiles, filters, chebs, us, own, arrived):
    (c0, c1, c2), (u0, u1, u2) = chebs, us
    sources = (*arrived, c2, c1, c0, own, u1, u2, u0)
    args = (*tables, tiles, filters, *sources)
    scratch = [pltpu.VMEM(a.shape, a.dtype) for a in sources]
    scratch += [pltpu.SemaphoreType.DMA((len(sources),))]
    scratch += [EXT, ACC, pltpu.VMEM((NB, C, BLK), F32)]
    scratch += [pltpu.VMEM((2, *BLOCKS.shape), BF16), pltpu.SemaphoreType.DMA((4,))]
    return call(
        end_kernel, "end", [BLOCKS, BLOCKS], [HBM] * 2,
        [SMEM] * 4 + [VMEM] * 2 + [HBM] * len(sources), scratch, END_FLOPS, args,
    )


def trade(letters):
    size = lax.axis_size(SKY)
    got = []
    for letter, kind in zip(letters, ROUNDS):
        pairs = [(i, partner_of(i, kind)) for i in range(size)]
        pairs = [(i, j) for i, j in pairs if 0 <= j < size]
        got.append(lax.ppermute(letter, SKY, pairs))
    return got


def fold_kernel(parts, out):
    members, rows = parts.shape[0], parts.shape[1]
    total = parts[0].astype(F32)
    for k in range(1, members):
        total = total + parts[k].astype(F32)
    total = total.astype(BF16)
    for k in range(members):
        out[k] = total


def total_over_devices(local):
    others = lax.axis_size("view") * lax.axis_size("z")
    rows = local.shape[0] // PLANE
    assert others == PLANE and rows % 16 == 0
    parts = local.reshape(PLANE, rows, C)
    for axes, flops in ((("plane",), END_FLOPS), (("view", "z"), 0)):
        parts = lax.all_to_all(parts, axes, 0, 0, tiled=True)
        shape = jax.ShapeDtypeStruct(parts.shape, BF16)
        parts = call(fold_kernel, "fold", [shape], [VMEM], [VMEM], [], flops, (parts,))[0]
    whole = lax.all_to_all(parts, ("plane",), 0, 0, tiled=True)
    return whole.reshape(4, C, C).astype(F32)


def per_device(
    pixels, cotangent, filters, lap_tiles, tile_target, tile_source, tile_count, send_blocks
):
    c0 = pixels.reshape(NB, BLK, C)
    upstream = cotangent.reshape(NB, BLK, C)
    tiles = lap_tiles.reshape(MAXT, BLK, BLK)
    tables = (tile_target, tile_source, tile_count, send_blocks.swapaxes(1, 2))
    scale = 1.0 / math.sqrt(lax.axis_size("view") * lax.axis_size(SKY) * NB * BLK)

    u0, own, tiles, *letters = start(tables, tiles, c0, upstream)
    arrived = trade(letters)
    c1, u1, own, *letters = first_step(tables, tiles, c0, own, arrived)
    arrived = trade(letters)
    c2, u2, own, *letters, local = second_step(tables, tiles, c1, own, arrived, scale, u0, c0, u1)
    filter_grad = total_over_devices(local)
    arrived = trade(letters)
    outputs, pixel_grad = end(tables, tiles, filters, (c0, c1, c2), (u0, u1, u2), own, arrived)
    return (outputs.reshape(pixels.shape), pixel_grad.reshape(pixels.shape), filter_grad)


def solution(mesh):
    views, skies = mesh.devices.shape
    fine = Mesh(mesh.devices.reshape(views, skies // PLANE, PLANE), ("view", *SKY))
    return jax.shard_map(
        per_device,
        mesh=fine,
        in_specs=(
            P("view", SKY, None),
            P("view", SKY, None),
            P(),
            P(SKY, None, None, None),
            P(SKY, None),
            P(SKY, None),
            P(SKY),
            P(SKY, None, None),
        ),
        out_specs=(P("view", SKY, None), P("view", SKY, None), P()),
        check_vma=False,
    )
```
